512 devices in a mesh: seq: 16 (over z, core), ctx: 32 (over y, x).
Axes of the slice: x: 4, y: 8, z: 8, core: 2. Of those that a mesh axis runs over, the one named last changes fastest.
Arguments:
- queries: bfloat16 [65536, 2048], P(('seq', 'ctx')), parts along dimension 0, may hold values from -6 to 6
- key_rows: bfloat16 [65536, 2048], P(('seq', 'ctx')), parts along dimension 0, may hold values from -6 to 6
- values: bfloat16 [65536, 2048], P(('seq', 'ctx')), parts along dimension 0, may hold values from -6 to 6
- out_grad: bfloat16 [65536, 2048], P(('seq', 'ctx')), parts along dimension 0, may hold values from -0.008239746 to 0.008239746
- feature_map: bfloat16 [16, 128, 128], replicated, may hold values from -0.5 to 0.5
Outputs:
- query_grad: bfloat16 [65536, 2048], P(('seq', 'ctx')), parts along dimension 0
- key_grad: bfloat16 [65536, 2048], P(('seq', 'ctx')), parts along dimension 0
- value_grad: bfloat16 [65536, 2048], P(('seq', 'ctx')), parts along dimension 0
- map_grad: float32 [256, 128, 128], P('seq'), parts along dimension 0
The draws below stay inside these ranges and needn't reach their ends.
There are 16 independent parts, one for each index of `seq`. The reference program is written for one: setup_inputs(seed, part) draws one part's arguments, and reference() takes and returns one part's arrays. A program takes and returns all parts, laid end to end along the dimension named above; an argument that names none is the same for every part. Nothing has to cross between parts.
All inputs are finite; a program needn't handle non-finite values.
Results may differ from the reference program's by a relative error of at most 0.033.
Values may be sent and summed in bfloat16 or wider, within the bound.
A program may use at most 128 MiB of HBM per device.

```python
import math
import jax
import jax.numpy as jnp
from jax import lax

HEADS = 16
HD = 128
TOK_DEV = 128
TOKENS = 4096
N_CTX = 32


def steps_of(stream_key, extent, cuts, smallest, high):
    def one(axis_at, parts):
        steps = jax.random.uniform(jax.random.fold_in(jax.random.fold_in(stream_key, 6), axis_at), (parts,), jnp.float32, smallest / len(cuts), high / len(cuts))
        return jnp.repeat(jnp.exp(steps), extent[axis_at] // parts).reshape((-1,) + (1,) * (len(extent) - axis_at - 1))

    loudness = one(*cuts[0])
    for cut in cuts[1:]:
        loudness = loudness * one(*cut)
    return loudness


def centred(key, extent, deviation, most, shards=(), dtype=jnp.bfloat16):
    loudness = steps_of(key, extent, shards, -0.22, 0.18) if shards else 1.0
    drawn = jax.random.normal(key, extent, jnp.float32) * deviation * loudness
    return jnp.minimum(jnp.maximum(drawn, -most), most).astype(dtype)


def setup_inputs(seed: int = 0, part: int = 0) -> dict:
    keys = jax.random.split(jax.random.key(seed), 6)
    part_splits = jax.random.split(jax.random.fold_in(keys[5], part), 6)
    return {
        "queries": centred(part_splits[0], (TOKENS, HEADS * HD), 1.0, 6.0, ((0, 32),)),
        "key_rows": centred(part_splits[1], (TOKENS, HEADS * HD), 1.0, 6.0, ((0, 32),)),
        "values": centred(part_splits[2], (TOKENS, HEADS * HD), 1.0, 6.0, ((0, 32),)),
        "out_grad": centred(part_splits[3], (TOKENS, HEADS * HD), ((HD * TOKENS) ** -0.5), 0.008239746, ((0, 32),)),
        "feature_map": centred(keys[4], (HEADS, HD, HD), HD ** -0.5, 0.5),
    }


def rounded(x):
    return lax.optimization_barrier(x.astype(jnp.bfloat16)).astype(jnp.float32)

def reference(queries, key_rows, values, out_grad, feature_map):
    f32 = jnp.float32

    def split(x):
        return x.astype(f32).reshape(N_CTX, TOK_DEV, HEADS, HD)
    query_h = split(queries)
    key_h = split(key_rows)
    value_h = split(values)
    grad_h = split(out_grad)
    weights = feature_map.astype(f32)
    query_feat = rounded(jnp.einsum('bthd,hde->bthe', query_h, weights))
    key_feat = rounded(jnp.einsum('bthd,hde->bthe', key_h, weights))
    key_state = rounded(jnp.einsum('bthe,bthv->bhev', key_feat, value_h))
    grad_state = rounded(jnp.einsum('bthe,bthv->bhev', query_feat, grad_h))
    empty = jnp.zeros_like(key_state[:1])
    prefix = jnp.concatenate([empty, jnp.cumsum(key_state, 0)[:-1]], 0)
    backward = jnp.cumsum(grad_state[::-1], 0)[::-1]
    suffix = jnp.concatenate([backward[1:], empty], 0)
    prefix = rounded(prefix)
    suffix = rounded(suffix)
    rows_idx = lax.broadcasted_iota(jnp.int32, (TOK_DEV, TOK_DEV), 0)
    cols_idx = lax.broadcasted_iota(jnp.int32, (TOK_DEV, TOK_DEV), 1)
    causal = rows_idx >= cols_idx
    scores = jnp.einsum('bthe,bshe->bhts', query_feat, key_feat)
    scores = rounded(jnp.where(causal, scores, 0.0))
    mixing = jnp.einsum('bthv,bshv->bhts', grad_h, value_h)
    mixing = rounded(jnp.where(causal, mixing, 0.0))
    feat_qgrad = rounded(jnp.einsum('bhts,bshe->bthe', mixing, key_feat) + jnp.einsum('bthv,bhev->bthe', grad_h, prefix))
    feat_kgrad = rounded(jnp.einsum('bhts,bthe->bshe', mixing, query_feat) + jnp.einsum('bshv,bhev->bshe', value_h, suffix))
    value_grad = jnp.einsum('bhts,bthv->bshv', scores, grad_h) + jnp.einsum('bshe,bhev->bshv', key_feat, suffix)
    query_grad = jnp.einsum('bthe,hde->bthd', feat_qgrad, weights)
    key_grad = jnp.einsum('bthe,hde->bthd', feat_kgrad, weights)
    block_mgrad = jnp.einsum('bthd,bthe->bhde', query_h, feat_qgrad) + jnp.einsum('bthd,bthe->bhde', key_h, feat_kgrad)
    block_mgrad = rounded(block_mgrad)
    map_grad = lax.optimization_barrier(jnp.sum(block_mgrad, 0)) / math.sqrt(TOKENS)
    whole = (TOKENS, HEADS * HD)
    return (query_grad.reshape(whole).astype(jnp.bfloat16), key_grad.reshape(whole).astype(jnp.bfloat16), value_grad.reshape(whole).astype(jnp.bfloat16), map_grad.astype(f32))
```

```python
import functools

import jax
import jax.numpy as jnp
from jax import lax
from jax.experimental import pallas as pl
from jax.experimental.pallas import tpu as pltpu
from jax.sharding import PartitionSpec as P

MESH = pl.DeviceIdType.MESH
F32 = jnp.float32
BF16 = jnp.bfloat16

NX = 4
NY = 8
HEADS = 16
QUARTER = HEADS // NX
CHUNKS = 2
PER = QUARTER // CHUNKS
HD = 128
OWNERS = (0, 4, 2, 6)


def mm(a, b, ca=1, cb=0):
    return lax.dot_general(a, b, (((ca,), (cb,)), ((), ())), preferred_element_type=F32)


def kernel(
    q_in, k_in, v_in, g_in, f_in,
    q_out, k_out, v_out, z_out,
    q, k, v, g, f, dq, dk, dv,
    sent, got, y_sent, y_got, total, z_row, w_row,
    col, col_z, carry, carried, w_col, z_all,
    out_send, fin, h_mat, kh, aq, ak, av,
    in_sem, out_sem, z_sem,
    p1s, p1r, ys, yr, p2s, p2r, z2s, z2r, p3s, p3r, z3s, z3r, p4s, p4r, z4s, z4r,
):
    me = lax.axis_index("ctx")
    y = me // NX
    x = lax.rem(me, NX)
    mine_j = lax.rem(y // 2, 2) * 2 + y // 4
    is_owner = lax.rem(y, 2) == 0

    def at_x(d):
        return lax.rem(x + d + NX, NX)

    def at_y(d):
        return lax.rem(y + d + NY, NY)

    def place(py, px):
        return {"ctx": py * NX + px}

    def remote(src, dst, ssem, rsem, py, px):
        return pltpu.make_async_remote_copy(
            src_ref=src, dst_ref=dst, send_sem=ssem, recv_sem=rsem,
            device_id=place(py, px), device_id_type=MESH,
        )

    loads = [
        pltpu.make_async_copy(a, b, in_sem.at[i])
        for i, (a, b) in enumerate(((k_in, k), (v_in, v), (q_in, q), (g_in, g), (f_in, f)))
    ]
    for load in loads:
        load.start()

    barrier = pltpu.get_barrier_semaphore()
    for d in range(1, NX):
        pl.semaphore_signal(barrier, inc=1, device_id=place(y, at_x(d)), device_id_type=MESH)
    for d in range(1, NY):
        pl.semaphore_signal(barrier, inc=1, device_id=place(at_y(d), x), device_id_type=MESH)
    for load in loads[:4]:
        load.wait()
    pl.semaphore_wait(barrier, NX + NY - 2)

    def cols(h):
        return pl.ds(pl.multiple_of(h * HD, HD), HD)

    def p1(c, d):
        js = pl.ds(c * PER, PER)
        return remote(sent.at[at_x(d), js], got.at[x, js], p1s.at[c, d - 1], p1r.at[c, d - 1], y, at_x(d))

    def p1_in(c, d):
        js = pl.ds(c * PER, PER)
        return remote(sent.at[at_x(d), js], got.at[at_x(-d), js], p1s.at[c, d - 1], p1r.at[c, d - 1], y, at_x(d))

    def py_(c, d):
        js = pl.ds(c * PER, PER)
        return remote(y_sent.at[at_x(d), js], y_got.at[x, js], ys.at[c, d - 1], yr.at[c, d - 1], y, at_x(d))

    def py_in(c, d):
        js = pl.ds(c * PER, PER)
        return remote(y_sent.at[at_x(d), js], y_got.at[at_x(-d), js], ys.at[c, d - 1], yr.at[c, d - 1], y, at_x(d))

    def p2(j):
        return remote(total.at[j], col.at[y], p2s.at[j], p2r.at[y], OWNERS[j], x)

    def p2_in(d):
        return remote(total.at[0], col.at[at_y(d)], p2s.at[0], p2r.at[at_y(d)], at_y(d), x)

    def z2(j):
        return remote(z_row.at[j], col_z.at[y], z2s.at[j], z2r.at[y], OWNERS[j], x)

    def z2_in(d):
        return remote(z_row.at[0], col_z.at[at_y(d)], z2s.at[0], z2r.at[at_y(d)], at_y(d), x)

    def p3(d):
        return remote(carry.at[at_y(d)], carried.at[mine_j], p3s.at[d - 1], p3r.at[mine_j], at_y(d), x)

    def p3_in(j):
        return remote(carry.at[0], carried.at[j], p3s.at[0], p3r.at[j], OWNERS[j], x)

    def z3(d):
        head = x * QUARTER + mine_j
        return remote(z_all.at[head], z_all.at[head], z3s.at[d - 1], z3r.at[mine_j], at_y(d), x)

    def z3_in(j):
        head = x * QUARTER + j
        return remote(z_all.at[head], z_all.at[head], z3s.at[0], z3r.at[j], OWNERS[j], x)

    def p4(c, d):
        return remote(
            out_send.at[at_x(d), pl.ds(c * PER, PER)], fin.at[pl.ds(x * QUARTER + c * PER, PER)],
            p4s.at[c, d - 1], p4r.at[c, d - 1], y, at_x(d),
        )

    def p4_in(c, d):
        return remote(
            out_send.at[at_x(d), pl.ds(c * PER, PER)], fin.at[pl.ds(at_x(-d) * QUARTER + c * PER, PER)],
            p4s.at[c, d - 1], p4r.at[c, d - 1], y, at_x(d),
        )

    def z4(c, d):
        hs = pl.ds(x * QUARTER + c * PER, PER)
        return remote(z_all.at[hs], z_all.at[hs], z4s.at[c, d - 1], z4r.at[c, d - 1], y, at_x(d))

    def z4_in(c, d):
        hs = pl.ds(at_x(-d) * QUARTER + c * PER, PER)
        return remote(z_all.at[hs], z_all.at[hs], z4s.at[c, d - 1], z4r.at[c, d - 1], y, at_x(d))

    order = (2, 1, 3)
    for c in range(CHUNKS):
        for d in order + (0,):
            xo = at_x(d)
            for j in range(c * PER, c * PER + PER):
                hc = cols(xo * QUARTER + j)
                ks = mm(v[:, hc], k[:, hc], 0, 0).astype(BF16)
                gs = mm(q[:, hc], g[:, hc], 0, 0).astype(BF16)
                if d:
                    sent[xo, j, 0] = ks
                    sent[xo, j, 1] = gs
                else:
                    got[x, j, 0] = ks
                    got[x, j, 1] = gs
            if d:
                p1(c, d).start()

    loads[4].wait()
    rows = lax.broadcasted_iota(jnp.int32, (HD, HD), 0)
    columns = lax.broadcasted_iota(jnp.int32, (HD, HD), 1)
    lower = rows >= columns
    upper = rows <= columns

    def local(h):
        hc = cols(h)
        qh, kh_in, vh, gh = q[:, hc], k[:, hc], v[:, hc], g[:, hc]
        fh = f[h]
        hm = mm(fh, fh, 1, 1).astype(BF16)
        h_mat[h] = hm
        khm = mm(kh_in, hm).astype(BF16)
        kh[h] = khm
        scores_t = jnp.where(upper, mm(khm, qh, 1, 1), 0.0).astype(BF16)
        mixing = jnp.where(lower, mm(gh, vh, 1, 1), 0.0).astype(BF16)
        mixing_t = jnp.where(upper, mm(vh, gh, 1, 1), 0.0).astype(BF16)
        a = mm(mixing, kh_in)
        aq[h] = a
        ak[h] = mm(mixing_t, qh)
        av[h] = mm(scores_t, gh)
        return mm(qh, a.astype(BF16), 0, 0).astype(BF16)

    for c in range(CHUNKS):
        for d in order + (0,):
            xo = at_x(d)
            for j in range(c * PER, c * PER + PER):
                part = local(xo * QUARTER + j)
                if d:
                    y_sent[xo, j] = part
                else:
                    y_got[x, j] = part
            if d:
                py_(c, d).start()

    def sums(j):
        ks = [got[i, j, 0].astype(F32) for i in range(NX)]
        gs = [got[i, j, 1].astype(F32) for i in range(NX)]
        before = [None, ks[0]]
        for i in range(1, NX):
            before.append(before[-1] + ks[i])
        after = [None, gs[NX - 1]]
        for i in range(NX - 2, -1, -1):
            after.append(after[-1] + gs[i])
        return before, after

    for c in range(CHUNKS):
        for d in order:
            p1_in(c, d).wait_recv()
        for j in range(c * PER, c * PER + PER):
            before, after = sums(j)
            total[j, 0] = before[NX].astype(BF16)
            total[j, 1] = after[NX].astype(BF16)

            @pl.when(y != OWNERS[j])
            def _():
                p2(j).start()

            @pl.when(y == OWNERS[j])
            def _():
                col[y] = total[j]

            w = mm(got[1, j, 1], before[1].astype(BF16))
            for i in range(2, NX):
                w += mm(got[i, j, 1], before[i].astype(BF16))
            w_row[j] = w
    for c in range(CHUNKS):
        for d in order:
            py_in(c, d).wait_recv()
        for j in range(c * PER, c * PER + PER):
            w = w_row[j]
            for i in range(NX):
                w += y_got[i, j].astype(F32)
            z_row[j] = w.astype(BF16)

            @pl.when(y != OWNERS[j])
            def _():
                z2(j).start()

            @pl.when(y == OWNERS[j])
            def _():
                col_z[y] = z_row[j]

    for c in range(CHUNKS):

        @pl.when(is_owner & (mine_j // PER == c))
        def _():
            for d in range(1, NY):
                p2_in(d).wait_recv()
            acc = jnp.zeros((HD, HD), F32)
            w = jnp.zeros((HD, HD), F32)
            for i in range(NY):
                low = acc.astype(BF16)
                carry[i, 0] = low
                if i:
                    w += mm(col[i, 1], low)
                acc = acc + col[i, 0].astype(F32)
            acc = jnp.zeros((HD, HD), F32)
            for i in range(NY - 1, -1, -1):
                carry[i, 1] = acc.astype(BF16)
                acc = acc + col[i, 1].astype(F32)
            for d in (4, 3, 5, 2, 6, 1, 7):
                p3(d).start()
            carried[mine_j] = carry[y]
            for d in range(1, NY):
                z2_in(d).wait_recv()
            for i in range(NY):
                w += col_z[i].astype(F32)
            w = w + w.T
            z_all[x * QUARTER + mine_j] = w.astype(BF16)
            for d in (4, 3, 5, 2, 6, 1, 7):
                z3(d).start()

        for j in range(c * PER, c * PER + PER):

            @pl.when(y != OWNERS[j])
            def _():
                p3_in(j).wait_recv()

            before, after = sums(j)
            pre = carried[j, 0].astype(F32)
            suf = carried[j, 1].astype(F32)
            for i in range(NX):
                out_send[i, j, 0] = (pre if i == 0 else pre + before[i]).astype(BF16)
                back = NX - 1 - i
                out_send[i, j, 1] = (suf if back == 0 else suf + after[back]).astype(BF16)
        for d in order:
            p4(c, d).start()
        fin[pl.ds(x * QUARTER + c * PER, PER)] = out_send[x, pl.ds(c * PER, PER)]
        for j in range(c * PER, c * PER + PER):

            @pl.when(y != OWNERS[j])
            def _():
                z3_in(j).wait_recv()

        for d in order:
            z4(c, d).start()

    def finish(h):
        hc = cols(h)
        pre_t = fin[h, 0]
        suf = fin[h, 1]
        hm = h_mat[h]
        a = (aq[h] + mm(g[:, hc], pre_t)).astype(BF16)
        dq[:, hc] = mm(a, hm).astype(BF16)
        b = (ak[h] + mm(v[:, hc], suf, 1, 1)).astype(BF16)
        dk[:, hc] = mm(b, hm).astype(BF16)
        dv[:, hc] = (av[h] + mm(kh[h], suf)).astype(BF16)

    outs = []
    for c in range(CHUNKS):
        for n, d in enumerate((0, 1, 3, 2)):
            if d:
                p4_in(c, d).wait_recv()
            xo = at_x(-d)
            for j in range(c * PER, c * PER + PER):
                finish(xo * QUARTER + j)
            part = pl.ds(pl.multiple_of((xo * QUARTER + c * PER) * HD, PER * HD), PER * HD)
            for i, (a, b) in enumerate(((dq, q_out), (dk, k_out), (dv, v_out))):
                copy = pltpu.make_async_copy(a.at[:, part], b.at[:, part], out_sem.at[c, n, i])
                copy.start()
                outs.append(copy)
    for c in range(CHUNKS):
        for d in order:
            z4_in(c, d).wait_recv()
    z_copy = pltpu.make_async_copy(z_all, z_out, z_sem)
    z_copy.start()

    for c in range(CHUNKS):
        for d in order:
            p1(c, d).wait_send()
            py_(c, d).wait_send()
            p4(c, d).wait_send()
            z4(c, d).wait_send()
    for j in range(QUARTER):

        @pl.when(y != OWNERS[j])
        def _():
            p2(j).wait_send()
            z2(j).wait_send()

    @pl.when(is_owner)
    def _():
        for d in range(1, NY):
            p3(d).wait_send()
            z3(d).wait_send()

    for copy in outs:
        copy.wait()
    z_copy.wait()


def per_device(queries, key_rows, values, out_grad, feature_map):
    tokens, width = queries.shape
    dma = pltpu.SemaphoreType.DMA
    state = (HD, HD)
    flat = jax.ShapeDtypeStruct((tokens, width), BF16)
    rows = (tokens, width)
    query_grad, key_grad, value_grad, z = pl.pallas_call(
        kernel,
        out_shape=(flat, flat, flat, jax.ShapeDtypeStruct((HEADS,) + state, BF16)),
        in_specs=[pl.BlockSpec(memory_space=pl.ANY)] * 5,
        out_specs=[pl.BlockSpec(memory_space=pl.ANY)] * 4,
        scratch_shapes=[
            pltpu.VMEM(rows, BF16), pltpu.VMEM(rows, BF16), pltpu.VMEM(rows, BF16), pltpu.VMEM(rows, BF16),
            pltpu.VMEM((HEADS,) + state, BF16),
            pltpu.VMEM(rows, BF16), pltpu.VMEM(rows, BF16), pltpu.VMEM(rows, BF16),
            pltpu.VMEM((NX, QUARTER, 2) + state, BF16),
            pltpu.VMEM((NX, QUARTER, 2) + state, BF16),
            pltpu.VMEM((NX, QUARTER) + state, BF16),
            pltpu.VMEM((NX, QUARTER) + state, BF16),
            pltpu.VMEM((QUARTER, 2) + state, BF16),
            pltpu.VMEM((QUARTER,) + state, BF16),
            pltpu.VMEM((QUARTER,) + state, F32),
            pltpu.VMEM((NY, 2) + state, BF16),
            pltpu.VMEM((NY,) + state, BF16),
            pltpu.VMEM((NY, 2) + state, BF16),
            pltpu.VMEM((QUARTER, 2) + state, BF16),
            pltpu.VMEM(state, F32),
            pltpu.VMEM((HEADS,) + state, BF16),
            pltpu.VMEM((NX, QUARTER, 2) + state, BF16),
            pltpu.VMEM((HEADS, 2) + state, BF16),
            pltpu.VMEM((HEADS,) + state, BF16),
            pltpu.VMEM((HEADS,) + state, BF16),
            pltpu.VMEM((HEADS,) + state, F32), pltpu.VMEM((HEADS,) + state, F32), pltpu.VMEM((HEADS,) + state, F32),
            dma((5,)), dma((CHUNKS, NX, 3)), dma,
            dma((CHUNKS, 3)), dma((CHUNKS, 3)), dma((CHUNKS, 3)), dma((CHUNKS, 3)),
            dma((QUARTER,)), dma((NY,)), dma((QUARTER,)), dma((NY,)),
            dma((NY - 1,)), dma((QUARTER,)), dma((NY - 1,)), dma((QUARTER,)),
            dma((CHUNKS, 3)), dma((CHUNKS, 3)), dma((CHUNKS, 3)), dma((CHUNKS, 3)),
        ],
        compiler_params=pltpu.CompilerParams(
            collective_id=0, has_side_effects=True, vmem_limit_bytes=48 * 1024 * 1024
        ),
    )(queries, key_rows, values, out_grad, feature_map)
    map_grad = jnp.einsum("hcd,hde->hce", z, feature_map, preferred_element_type=F32) * (
        1.0 / (tokens * lax.axis_size("ctx")) ** 0.5
    )
    return query_grad, key_grad, value_grad, map_grad


def solution(mesh):
    placed = P(("seq", "ctx"), None)
    return jax.shard_map(
        per_device,
        mesh=mesh,
        in_specs=(placed, placed, placed, placed, P()),
        out_specs=(placed, placed, placed, P("seq", None, None)),
        check_vma=False,
    )
```

```python
import functools
import math

import jax
import jax.numpy as jnp
from jax import lax
from jax.experimental import pallas as pl
from jax.experimental.pallas import tpu as pltpu
from jax.sharding import PartitionSpec as P

MESH = pl.DeviceIdType.MESH
F32 = jnp.float32
BF16 = jnp.bfloat16

NX = 4
NY = 8
HEADS = 16
QUARTER = HEADS // NX
CHUNKS = 4
PER = QUARTER // CHUNKS
HD = 128
SLICE = HD // NY


def mm(a, b, ca=1, cb=0):
    return lax.dot_general(a, b, (((ca,), (cb,)), ((), ())), preferred_element_type=F32)


def kernel(
    q_in, k_in, v_in, g_in, f_in,
    q_out, k_out, v_out, z_out,
    q, k, v, g, f, dq, dk, dv,
    sent, got, y_sent, y_got, total, col, carry, carried,
    w_row, z_row, col_z, z_part, z_full, z_all,
    out_send, fin, h_mat, kh, aq, ak, av,
    in_sem, out_sem, z_sem,
    p1s, p1r, ys, yr, p2s, p2r, p3s, p3r, p4s, p4r, z2s, z2r, z3s, z3r, z4s, z4r,
):
    me = lax.axis_index("ctx")
    y = me // NX
    x = lax.rem(me, NX)

    def at_x(d):
        return lax.rem(x + d + NX, NX)

    def at_y(d):
        return lax.rem(y + d + NY, NY)

    def place(py, px):
        return {"ctx": py * NX + px}

    loads = [
        pltpu.make_async_copy(a, b, in_sem.at[i])
        for i, (a, b) in enumerate(((k_in, k), (v_in, v), (q_in, q), (g_in, g), (f_in, f)))
    ]
    for load in loads:
        load.start()

    barrier = pltpu.get_barrier_semaphore()
    for d in range(1, NX):
        pl.semaphore_signal(barrier, inc=1, device_id=place(y, at_x(d)), device_id_type=MESH)
    for d in range(1, NY):
        pl.semaphore_signal(barrier, inc=1, device_id=place(at_y(d), x), device_id_type=MESH)
    for load in loads[:4]:
        load.wait()
    pl.semaphore_wait(barrier, NX + NY - 2)

    def cols(h, n=1):
        return pl.ds(pl.multiple_of(h * HD, HD), n * HD)

    def rows_of(i):
        return pl.ds(pl.multiple_of(i * SLICE, SLICE), SLICE)

    def heads_of(c):
        return range(c * PER, c * PER + PER)

    def along_x(src, dst, ssem, rsem, c, d, into):
        return pltpu.make_async_remote_copy(
            src_ref=src(at_x(d)), dst_ref=dst(at_x(-d) if into else x),
            send_sem=ssem.at[c, d - 1], recv_sem=rsem.at[c, d - 1],
            device_id=place(y, at_x(d)), device_id_type=MESH,
        )

    def along_y(src, dst, ssem, rsem, c, d, into):
        return pltpu.make_async_remote_copy(
            src_ref=src(at_y(d)), dst_ref=dst(at_y(-d) if into else y),
            send_sem=ssem.at[c, d - 1], recv_sem=rsem.at[c, d - 1],
            device_id=place(at_y(d), x), device_id_type=MESH,
        )

    def p1(c, d, into=False):
        js = pl.ds(c * PER, PER)
        return along_x(lambda i: sent.at[i, js], lambda i: got.at[i, js], p1s, p1r, c, d, into)

    def p_y(c, d, into=False):
        js = pl.ds(c * PER, PER)
        return along_x(lambda i: y_sent.at[i, js], lambda i: y_got.at[i, js], ys, yr, c, d, into)

    def p2(c, d, into=False):
        js = pl.ds(c * PER, PER)
        return along_y(lambda i: total.at[js, :, rows_of(i)], lambda i: col.at[i, js], p2s, p2r, c, d, into)

    def p3(c, d, into=False):
        js = pl.ds(c * PER, PER)
        return along_y(lambda i: carry.at[i, js], lambda i: carried.at[js, :, rows_of(i)], p3s, p3r, c, d, into)

    def p4(c, d, into=False):
        js = pl.ds(c * PER, PER)
        return along_x(
            lambda i: out_send.at[i, js], lambda i: fin.at[pl.ds(i * QUARTER + c * PER, PER)], p4s, p4r, c, d, into
        )

    def z2(c, d, into=False):
        js = pl.ds(c * PER, PER)
        return along_y(lambda i: z_row.at[js, rows_of(i)], lambda i: col_z.at[i, js], z2s, z2r, c, d, into)

    def z3(c, d, into=False):
        js = pl.ds(c * PER, PER)
        return along_y(lambda i: z_part.at[js], lambda i: z_full.at[js, rows_of(i)], z3s, z3r, c, d, into)

    def z4(c, d, into=False):
        def hs(i):
            return z_all.at[pl.ds(i * QUARTER + c * PER, PER)]

        return along_x(lambda i: hs(x), hs, z4s, z4r, c, d, into)

    x_order = (2, 1, 3)
    y_order = (4, 3, 5, 2, 6, 1, 7)

    def states(c, send=True):
        for d in x_order + (0,):
            xo = at_x(d)
            for j in heads_of(c):
                hc = cols(xo * QUARTER + j)
                ks = mm(v[:, hc], k[:, hc], 0, 0).astype(BF16)
                gs = mm(g[:, hc], q[:, hc], 0, 0).astype(BF16)
                if d:
                    sent[xo, j, 0] = ks
                    sent[xo, j, 1] = gs
                else:
                    got[x, j, 0] = ks
                    got[x, j, 1] = gs
            if d and send:
                p1(c, d).start()

    def send_states(c):
        for d in x_order:
            p1(c, d).start()

    rows = lax.broadcasted_iota(jnp.int32, (HD, HD), 0)
    columns = lax.broadcasted_iota(jnp.int32, (HD, HD), 1)
    lower = rows >= columns
    upper = rows <= columns

    def local(h):
        hc = cols(h)
        qh, kh_in, vh, gh = q[:, hc], k[:, hc], v[:, hc], g[:, hc]
        fh = f[h]
        hm = mm(fh, fh, 1, 1).astype(BF16)
        h_mat[h] = hm
        khm = mm(kh_in, hm).astype(BF16)
        kh[h] = khm
        scores_t = jnp.where(upper, mm(khm, qh, 1, 1), 0.0).astype(BF16)
        mixing = jnp.where(lower, mm(gh, vh, 1, 1), 0.0).astype(BF16)
        mixing_t = jnp.where(upper, mm(vh, gh, 1, 1), 0.0).astype(BF16)
        a = mm(mixing, kh_in)
        aq[h] = a
        ak[h] = mm(mixing_t, qh)
        av[h] = mm(scores_t, gh)
        return mm(qh, a.astype(BF16), 0, 0).astype(BF16)

    def block_work(c, d):
        xo = at_x(d)
        for j in heads_of(c):
            part = local(xo * QUARTER + j)
            if d:
                y_sent[xo, j] = part
            else:
                y_got[x, j] = part

    def send_y(c):
        for d in x_order:
            p_y(c, d).start()

    def sums(j):
        ks = [got[i, j, 0].astype(F32) for i in range(NX)]
        gs = [got[i, j, 1].astype(F32) for i in range(NX)]
        before = [None, ks[0]]
        for i in range(1, NX):
            before.append(before[-1] + ks[i])
        after = [None, gs[NX - 1]]
        for i in range(NX - 2, -1, -1):
            after.append(after[-1] + gs[i])
        return before, after

    def row_sums(c):
        for d in x_order:
            p1(c, d, True).wait_recv()
        for j in heads_of(c):
            before, after = sums(j)
            total[j, 0] = before[NX].astype(BF16)
            total[j, 1] = after[NX].astype(BF16)
            col[y, j] = total[j, :, rows_of(y)]
        for d in y_order:
            p2(c, d).start()

    def scan(c):
        for d in y_order:
            p2(c, d, True).wait_recv()
        for j in heads_of(c):
            acc = jnp.zeros((SLICE, HD), F32)
            for i in range(NY):
                carry[i, j, 0] = acc.astype(BF16)
                acc = acc + col[i, j, 0].astype(F32)
            acc = jnp.zeros((SLICE, HD), F32)
            for i in range(NY - 1, -1, -1):
                carry[i, j, 1] = acc.astype(BF16)
                acc = acc + col[i, j, 1].astype(F32)
            carried[j, :, rows_of(y)] = carry[y, j]
        for d in y_order:
            p3(c, d).start()

    def row_back(c):
        for d in y_order:
            p3(c, d, True).wait_recv()
        for j in heads_of(c):
            before, after = sums(j)
            pre = carried[j, 0].astype(F32)
            suf = carried[j, 1].astype(F32)
            for i in range(NX):
                out_send[i, j, 0] = (pre if i == 0 else pre + before[i]).astype(BF16)
                back = NX - 1 - i
                out_send[i, j, 1] = (suf if back == 0 else suf + after[back]).astype(BF16)
        for d in x_order:
            p4(c, d).start()
        fin[pl.ds(x * QUARTER + c * PER, PER)] = out_send[x, pl.ds(c * PER, PER)]

    def row_w(c):
        for j in heads_of(c):
            before, _ = sums(j)
            w = mm(got[1, j, 1], before[1].astype(BF16), 0, 0)
            for i in range(2, NX):
                w += mm(got[i, j, 1], before[i].astype(BF16), 0, 0)
            w_row[j] = w

    def row_z(c):
        for d in x_order:
            p_y(c, d, True).wait_recv()
        for j in heads_of(c):
            later = col[:, j, 1].reshape(HD, HD)
            w = w_row[j] + mm(later, carry[:, j, 0].reshape(HD, HD), 0, 0)
            for i in range(NX):
                w += y_got[i, j].astype(F32)
            z_row[j] = w.astype(BF16)
            col_z[y, j] = z_row[j, rows_of(y)]
        for d in y_order:
            z2(c, d).start()

    def col_z_sum(c):
        for d in y_order:
            z2(c, d, True).wait_recv()
        for j in heads_of(c):
            w = col_z[0, j].astype(F32)
            for i in range(1, NY):
                w += col_z[i, j].astype(F32)
            z_part[j] = w.astype(BF16)
            z_full[j, rows_of(y)] = z_part[j]
        for d in y_order:
            z3(c, d).start()

    def row_z_back(c):
        for d in y_order:
            z3(c, d, True).wait_recv()
        for j in heads_of(c):
            w = z_full[j].astype(F32)
            z_all[x * QUARTER + j] = (w + w.T).astype(BF16)
        for d in x_order:
            z4(c, d).start()

    def finish_head(h):
        hc = cols(h)
        pre_t = fin[h, 0]
        suf = fin[h, 1]
        hm = h_mat[h]
        a = (aq[h] + mm(g[:, hc], pre_t)).astype(BF16)
        dq[:, hc] = mm(a, hm).astype(BF16)
        b = (ak[h] + mm(v[:, hc], suf)).astype(BF16)
        dk[:, hc] = mm(b, hm).astype(BF16)
        dv[:, hc] = (av[h] + mm(kh[h], suf, 1, 1)).astype(BF16)

    outs = []

    def finish(c):
        for n, d in enumerate((0, 1, 3, 2)):
            if d:
                p4(c, d, True).wait_recv()
            xo = at_x(-d)
            for j in heads_of(c):
                finish_head(xo * QUARTER + j)
            part = cols(xo * QUARTER + c * PER, PER)
            for i, (a, b) in enumerate(((dq, q_out), (dk, k_out), (dv, v_out))):
                copy = pltpu.make_async_copy(a.at[:, part], b.at[:, part], out_sem.at[c, n, i])
                copy.start()
                outs.append(copy)

    blocks = [(c, d) for c in range(CHUNKS) for d in x_order + (0,)]

    def block_span(lo, hi):
        for c, d in blocks[lo:hi]:
            block_work(c, d)

    states(0)
    states(1, False)
    states(2, False)
    states(3, False)
    loads[4].wait()
    block_span(0, 1)
    send_states(1)
    block_span(1, 5)
    send_states(2)
    row_sums(0)
    block_span(5, 8)
    send_states(3)
    row_sums(1)
    block_span(8, 12)
    scan(0)
    row_sums(2)
    send_y(0)
    block_span(12, 14)
    send_y(1)
    scan(1)
    row_sums(3)
    send_y(2)
    block_span(14, 16)
    send_y(3)
    row_back(0)
    scan(2)
    row_w(0)
    row_z(0)
    row_back(1)
    scan(3)
    row_w(1)
    row_z(1)
    row_w(2)
    row_z(2)
    row_w(3)
    row_z(3)
    row_back(2)
    col_z_sum(0)
    row_back(3)
    col_z_sum(1)
    finish(0)
    col_z_sum(2)
    col_z_sum(3)
    row_z_back(0)
    finish(1)
    row_z_back(1)
    finish(2)
    row_z_back(2)
    row_z_back(3)
    finish(3)
    for c in range(CHUNKS):
        for d in x_order:
            z4(c, d, True).wait_recv()
    z_copy = pltpu.make_async_copy(z_all, z_out, z_sem)
    z_copy.start()

    for c in range(CHUNKS):
        for d in x_order:
            for p in (p1, p_y, p4, z4):
                p(c, d).wait_send()
        for d in y_order:
            for p in (p2, p3, z2, z3):
                p(c, d).wait_send()
    for copy in outs:
        copy.wait()
    z_copy.wait()


def emit(q_in, k_in, v_in, z, f, q_out, k_out, v_out, m_out, m, sem, m_sem, scale):
    copies = [
        pltpu.make_async_copy(a, b, sem.at[i])
        for i, (a, b) in enumerate(((q_in, q_out), (k_in, k_out), (v_in, v_out)))
    ]
    for copy in copies:
        copy.start()
    for part in range(4):
        for h in range(4 * part, 4 * part + 4):
            m[h] = mm(z[h], f[h]) * scale
        hs = pl.ds(4 * part, 4)
        copy = pltpu.make_async_copy(m.at[hs], m_out.at[hs], m_sem.at[part])
        copy.start()
        copies.append(copy)
    for copy in copies:
        copy.wait()


def per_device(queries, key_rows, values, out_grad, feature_map):
    tokens, width = queries.shape
    dma = pltpu.SemaphoreType.DMA
    state = (HD, HD)
    flat = jax.ShapeDtypeStruct((tokens, width), BF16)
    rows = (tokens, width)
    query_grad, key_grad, value_grad, z = pl.pallas_call(
        kernel,
        out_shape=(flat, flat, flat, jax.ShapeDtypeStruct((HEADS,) + state, BF16)),
        in_specs=[pl.BlockSpec(memory_space=pltpu.HBM)] * 5,
        out_specs=[pl.BlockSpec(memory_space=pl.ANY)] * 4,
        scratch_shapes=[
            pltpu.VMEM(rows, BF16), pltpu.VMEM(rows, BF16), pltpu.VMEM(rows, BF16), pltpu.VMEM(rows, BF16),
            pltpu.VMEM((HEADS,) + state, BF16),
            pltpu.VMEM(rows, BF16), pltpu.VMEM(rows, BF16), pltpu.VMEM(rows, BF16),
            pltpu.VMEM((NX, QUARTER, 2) + state, BF16),
            pltpu.VMEM((NX, QUARTER, 2) + state, BF16),
            pltpu.VMEM((NX, QUARTER) + state, BF16),
            pltpu.VMEM((NX, QUARTER) + state, BF16),
            pltpu.VMEM((QUARTER, 2) + state, BF16),
            pltpu.VMEM((NY, QUARTER, 2, SLICE, HD), BF16),
            pltpu.VMEM((NY, QUARTER, 2, SLICE, HD), BF16),
            pltpu.VMEM((QUARTER, 2) + state, BF16),
            pltpu.VMEM((QUARTER,) + state, F32),
            pltpu.VMEM((QUARTER,) + state, BF16),
            pltpu.VMEM((NY, QUARTER, SLICE, HD), BF16),
            pltpu.VMEM((QUARTER, SLICE, HD), BF16),
            pltpu.VMEM((QUARTER,) + state, BF16),
            pltpu.VMEM((HEADS,) + state, BF16),
            pltpu.VMEM((NX, QUARTER, 2) + state, BF16),
            pltpu.VMEM((HEADS, 2) + state, BF16),
            pltpu.VMEM((HEADS,) + state, BF16),
            pltpu.VMEM((HEADS,) + state, BF16),
            pltpu.VMEM((HEADS,) + state, F32), pltpu.VMEM((HEADS,) + state, F32), pltpu.VMEM((HEADS,) + state, F32),
            dma((5,)), dma((CHUNKS, NX, 3)), dma,
            *[dma((CHUNKS, NX - 1))] * 4,
            *[dma((CHUNKS, NY - 1))] * 4,
            *[dma((CHUNKS, NX - 1))] * 2,
            *[dma((CHUNKS, NY - 1))] * 4,
            *[dma((CHUNKS, NX - 1))] * 2,
        ],
        compiler_params=pltpu.CompilerParams(
            collective_id=0, has_side_effects=True, vmem_limit_bytes=48 * 1024 * 1024
        ),
    )(*(pltpu.with_memory_space_constraint(a, pltpu.HBM) for a in (queries, key_rows, values, out_grad, feature_map)))
    whole = pl.BlockSpec(memory_space=pltpu.VMEM)
    return pl.pallas_call(
        functools.partial(emit, scale=1.0 / math.sqrt(tokens * lax.axis_size("ctx"))),
        out_shape=(flat, flat, flat, jax.ShapeDtypeStruct((HEADS,) + state, F32)),
        in_specs=[pl.BlockSpec(memory_space=pl.ANY)] * 3 + [whole] * 2,
        out_specs=[pl.BlockSpec(memory_space=pl.ANY)] * 4,
        scratch_shapes=[pltpu.VMEM((HEADS,) + state, F32), dma((3,)), dma((4,))],
        compiler_params=pltpu.CompilerParams(vmem_limit_bytes=8 * 1024 * 1024),
    )(query_grad, key_grad, value_grad, z, feature_map)


def solution(mesh):
    placed = P(("seq", "ctx"), None)
    return jax.shard_map(
        per_device,
        mesh=mesh,
        in_specs=(placed, placed, placed, placed, P()),
        out_specs=(placed, placed, placed, P("seq", None, None)),
        check_vma=False,
    )
```

```python
import functools
import math

import jax
import jax.numpy as jnp
from jax import lax
from jax.experimental import pallas as pl
from jax.experimental.pallas import tpu as pltpu
from jax.sharding import PartitionSpec as P

MESH = pl.DeviceIdType.MESH
F32 = jnp.float32
BF16 = jnp.bfloat16

NX = 4
NY = 8
HEADS = 16
QUARTER = HEADS // NX
CHUNKS = 4
COLUMN_FIRST = (0, 1, )
PER = QUARTER // CHUNKS
HD = 128
SLICE = HD // NY


def mm(a, b, ca=1, cb=0):
    return lax.dot_general(a, b, (((ca,), (cb,)), ((), ())), preferred_element_type=F32)


def kernel(
    q_in, k_in, v_in, g_in, f_in,
    q_out, k_out, v_out, z_out,
    q, k, v, g, f, dq, dk, dv,
    sent, got, y_sent, y_got, total, col, carry, carried,
    w_row, z_row, col_z, z_part, z_full, z_all, y_col, y_sum, y_part,
    out_send, fin, h_mat, kh, aq, ak, av,
    in_sem, out_sem, z_sem,
    p1s, p1r, ys, yr, p2s, p2r, p3s, p3r, p4s, p4r, z2s, z2r, z3s, z3r, z4s, z4r, ycs, ycr, yxs, yxr,
):
    me = lax.axis_index("ctx")
    y = me // NX
    x = lax.rem(me, NX)

    def at_x(d):
        return lax.rem(x + d + NX, NX)

    def at_y(d):
        return lax.rem(y + d + NY, NY)

    def place(py, px):
        return {"ctx": py * NX + px}

    loads = [
        pltpu.make_async_copy(a, b, in_sem.at[i])
        for i, (a, b) in enumerate(((k_in, k), (v_in, v), (q_in, q), (g_in, g), (f_in, f)))
    ]
    for load in loads:
        load.start()

    barrier = pltpu.get_barrier_semaphore()
    for d in range(1, NX):
        pl.semaphore_signal(barrier, inc=1, device_id=place(y, at_x(d)), device_id_type=MESH)
    for d in range(1, NY):
        pl.semaphore_signal(barrier, inc=1, device_id=place(at_y(d), x), device_id_type=MESH)
    for load in loads[:4]:
        load.wait()
    pl.semaphore_wait(barrier, NX + NY - 2)

    def cols(h, n=1):
        return pl.ds(pl.multiple_of(h * HD, HD), n * HD)

    def rows_of(i):
        return pl.ds(pl.multiple_of(i * SLICE, SLICE), SLICE)

    def heads_of(c):
        return range(c * PER, c * PER + PER)

    def along_x(src, dst, ssem, rsem, c, d, into):
        return pltpu.make_async_remote_copy(
            src_ref=src(at_x(d)), dst_ref=dst(at_x(-d) if into else x),
            send_sem=ssem.at[c, d - 1], recv_sem=rsem.at[c, d - 1],
            device_id=place(y, at_x(d)), device_id_type=MESH,
        )

    def along_y(src, dst, ssem, rsem, c, d, into):
        return pltpu.make_async_remote_copy(
            src_ref=src(at_y(d)), dst_ref=dst(at_y(-d) if into else y),
            send_sem=ssem.at[c, d - 1], recv_sem=rsem.at[c, d - 1],
            device_id=place(at_y(d), x), device_id_type=MESH,
        )

    def p1(c, d, into=False):
        js = pl.ds(c * PER, PER)
        return along_x(lambda i: sent.at[i, js], lambda i: got.at[i, js], p1s, p1r, c, d, into)

    def p_y(c, d, into=False):
        js = pl.ds(c * PER, PER)
        return along_x(lambda i: y_sent.at[i, js], lambda i: y_got.at[i, js], ys, yr, c, d, into)

    def p2(c, d, into=False):
        js = pl.ds(c * PER, PER)
        return along_y(lambda i: total.at[js, :, rows_of(i)], lambda i: col.at[i, js], p2s, p2r, c, d, into)

    def p3(c, d, into=False):
        js = pl.ds(c * PER, PER)
        return along_y(lambda i: carry.at[i, js], lambda i: carried.at[js, :, rows_of(i)], p3s, p3r, c, d, into)

    def p4(c, d, into=False):
        js = pl.ds(c * PER, PER)
        return along_x(
            lambda i: out_send.at[i, js], lambda i: fin.at[pl.ds(i * QUARTER + c * PER, PER)], p4s, p4r, c, d, into
        )

    def z2(c, d, into=False):
        js = pl.ds(c * PER, PER)
        return along_y(lambda i: z_row.at[js, rows_of(i)], lambda i: col_z.at[i, js], z2s, z2r, c, d, into)

    def z3(c, d, into=False):
        js = pl.ds(c * PER, PER)
        return along_y(lambda i: z_part.at[js], lambda i: z_full.at[js, rows_of(i)], z3s, z3r, c, d, into)

    def z4(c, d, into=False):
        def hs(i):
            return z_all.at[pl.ds(i * QUARTER + c * PER, PER)]

        return along_x(lambda i: hs(x), hs, z4s, z4r, c, d, into)

    def y_down(c, d, into=False):
        js = pl.ds(c * PER, PER)
        return along_y(lambda i: y_sent.at[:, js, rows_of(i)], lambda i: y_col.at[i, :, js], ycs, ycr, c, d, into)

    def y_over(c, d, into=False):
        js = pl.ds(c * PER, PER)
        return along_x(lambda i: y_sum.at[i, js], lambda i: y_part.at[i, js], yxs, yxr, c, d, into)

    x_order = (2, 1, 3)
    y_order = (4, 3, 5, 2, 6, 1, 7)

    def states(c, send=True):
        for d in x_order + (0,):
            xo = at_x(d)
            for j in heads_of(c):
                hc = cols(xo * QUARTER + j)
                ks = mm(v[:, hc], k[:, hc], 0, 0).astype(BF16)
                gs = mm(g[:, hc], q[:, hc], 0, 0).astype(BF16)
                if d:
                    sent[xo, j, 0] = ks
                    sent[xo, j, 1] = gs
                else:
                    got[x, j, 0] = ks
                    got[x, j, 1] = gs
            if d and send:
                p1(c, d).start()

    def send_states(c):
        for d in x_order:
            p1(c, d).start()

    rows = lax.broadcasted_iota(jnp.int32, (HD, HD), 0)
    columns = lax.broadcasted_iota(jnp.int32, (HD, HD), 1)
    lower = rows >= columns
    upper = rows <= columns

    def local(h):
        hc = cols(h)
        qh, kh_in, vh, gh = q[:, hc], k[:, hc], v[:, hc], g[:, hc]
        fh = f[h]
        hm = mm(fh, fh, 1, 1).astype(BF16)
        h_mat[h] = hm
        khm = mm(kh_in, hm).astype(BF16)
        kh[h] = khm
        scores_t = jnp.where(upper, mm(khm, qh, 1, 1), 0.0).astype(BF16)
        mixing = jnp.where(lower, mm(gh, vh, 1, 1), 0.0).astype(BF16)
        mixing_t = jnp.where(upper, mm(vh, gh, 1, 1), 0.0).astype(BF16)
        a = mm(mixing, kh_in)
        aq[h] = a
        ak[h] = mm(mixing_t, qh)
        av[h] = mm(scores_t, gh)
        return mm(qh, a.astype(BF16), 0, 0).astype(BF16)

    def block_work(c, d):
        xo = at_x(d)
        for j in heads_of(c):
            part = local(xo * QUARTER + j)
            if d or c in COLUMN_FIRST:
                y_sent[xo, j] = part
            else:
                y_got[x, j] = part

    def send_y(c):
        if c in COLUMN_FIRST:
            for d in y_order:
                y_down(c, d).start()
            for j in heads_of(c):
                for i in range(NX):
                    y_col[y, i, j] = y_sent[i, j, rows_of(y)]
        else:
            for d in x_order:
                p_y(c, d).start()

    def column_y(c):
        for d in y_order:
            y_down(c, d, True).wait_recv()
        for j in heads_of(c):
            for i in range(NX):
                w = y_col[0, i, j].astype(F32)
                for n in range(1, NY):
                    w += y_col[n, i, j].astype(F32)
                y_sum[i, j] = w.astype(BF16)
            y_part[x, j] = y_sum[x, j]
        for d in x_order:
            y_over(c, d).start()

    def sums(j):
        ks = [got[i, j, 0].astype(F32) for i in range(NX)]
        gs = [got[i, j, 1].astype(F32) for i in range(NX)]
        before = [None, ks[0]]
        for i in range(1, NX):
            before.append(before[-1] + ks[i])
        after = [None, gs[NX - 1]]
        for i in range(NX - 2, -1, -1):
            after.append(after[-1] + gs[i])
        return before, after

    def row_sums(c):
        for d in x_order:
            p1(c, d, True).wait_recv()
        for j in heads_of(c):
            before, after = sums(j)
            total[j, 0] = before[NX].astype(BF16)
            total[j, 1] = after[NX].astype(BF16)
            col[y, j] = total[j, :, rows_of(y)]
        for d in y_order:
            p2(c, d).start()

    def scan(c):
        for d in y_order:
            p2(c, d, True).wait_recv()
        for j in heads_of(c):
            acc = jnp.zeros((SLICE, HD), F32)
            for i in range(NY):
                carry[i, j, 0] = acc.astype(BF16)
                acc = acc + col[i, j, 0].astype(F32)
            acc = jnp.zeros((SLICE, HD), F32)
            for i in range(NY - 1, -1, -1):
                carry[i, j, 1] = acc.astype(BF16)
                acc = acc + col[i, j, 1].astype(F32)
            carried[j, :, rows_of(y)] = carry[y, j]
        for d in y_order:
            p3(c, d).start()

    def row_back(c):
        for d in y_order:
            p3(c, d, True).wait_recv()
        for j in heads_of(c):
            before, after = sums(j)
            pre = carried[j, 0].astype(F32)
            suf = carried[j, 1].astype(F32)
            for i in range(NX):
                out_send[i, j, 0] = (pre if i == 0 else pre + before[i]).astype(BF16)
                back = NX - 1 - i
                out_send[i, j, 1] = (suf if back == 0 else suf + after[back]).astype(BF16)
        for d in x_order:
            p4(c, d).start()
        fin[pl.ds(x * QUARTER + c * PER, PER)] = out_send[x, pl.ds(c * PER, PER)]

    def row_w(c):
        for j in heads_of(c):
            before, _ = sums(j)
            w = mm(got[1, j, 1], before[1].astype(BF16), 0, 0)
            for i in range(2, NX):
                w += mm(got[i, j, 1], before[i].astype(BF16), 0, 0)
            w_row[j] = w

    def row_z(c):
        if c not in COLUMN_FIRST:
            for d in x_order:
                p_y(c, d, True).wait_recv()
        for j in heads_of(c):
            later = col[:, j, 1].reshape(HD, HD)
            w = w_row[j] + mm(later, carry[:, j, 0].reshape(HD, HD), 0, 0)
            if c not in COLUMN_FIRST:
                for i in range(NX):
                    w += y_got[i, j].astype(F32)
            z_row[j] = w.astype(BF16)
            col_z[y, j] = z_row[j, rows_of(y)]
        for d in y_order:
            z2(c, d).start()

    def col_z_sum(c):
        for d in y_order:
            z2(c, d, True).wait_recv()
        if c in COLUMN_FIRST:
            for d in x_order:
                y_over(c, d, True).wait_recv()
        for j in heads_of(c):
            w = col_z[0, j].astype(F32)
            for i in range(1, NY):
                w += col_z[i, j].astype(F32)
            if c in COLUMN_FIRST:
                for i in range(NX):
                    w += y_part[i, j].astype(F32)
            z_part[j] = w.astype(BF16)
            z_full[j, rows_of(y)] = z_part[j]
        for d in y_order:
            z3(c, d).start()

    def row_z_back(c):
        for d in y_order:
            z3(c, d, True).wait_recv()
        for j in heads_of(c):
            w = z_full[j].astype(F32)
            z_all[x * QUARTER + j] = (w + w.T).astype(BF16)
        for d in x_order:
            z4(c, d).start()

    def finish_head(h):
        hc = cols(h)
        pre_t = fin[h, 0]
        suf = fin[h, 1]
        hm = h_mat[h]
        a = (aq[h] + mm(g[:, hc], pre_t)).astype(BF16)
        dq[:, hc] = mm(a, hm).astype(BF16)
        b = (ak[h] + mm(v[:, hc], suf)).astype(BF16)
        dk[:, hc] = mm(b, hm).astype(BF16)
        dv[:, hc] = (av[h] + mm(kh[h], suf, 1, 1)).astype(BF16)

    outs = []

    def finish(c):
        places = (0, 1, 3, 2)
        for d in places[1:]:
            p4(c, d, True).wait_recv()
        for d in places:
            for j in heads_of(c):
                finish_head(at_x(-d) * QUARTER + j)
        for n, d in enumerate(places):
            part = cols(at_x(-d) * QUARTER + c * PER, PER)
            for i, (a, b) in enumerate(((dq, q_out), (dk, k_out), (dv, v_out))):
                copy = pltpu.make_async_copy(a.at[:, part], b.at[:, part], out_sem.at[c, n, i])
                copy.start()
                outs.append(copy)

    blocks = [(c, d) for c in range(CHUNKS) for d in x_order + (0,)]

    def block_span(lo, hi):
        for c, d in blocks[lo:hi]:
            block_work(c, d)

    states(0)
    states(1, False)
    states(2, False)
    states(3, False)
    loads[4].wait()
    block_span(0, 1)
    send_states(1)
    block_span(1, 4)
    send_y(0)
    block_span(4, 5)
    send_states(2)
    row_sums(0)
    block_span(5, 8)
    send_states(3)
    row_sums(1)
    send_y(1)
    block_span(8, 12)
    scan(0)
    row_sums(2)
    block_span(12, 14)
    column_y(0)
    scan(1)
    row_sums(3)
    send_y(2)
    block_span(14, 16)
    send_y(3)
    row_back(0)
    column_y(1)
    scan(2)
    row_w(0)
    row_z(0)
    row_back(1)
    scan(3)
    row_w(1)
    row_z(1)
    row_w(2)
    row_z(2)
    row_w(3)
    row_z(3)
    row_back(2)
    col_z_sum(0)
    row_back(3)
    col_z_sum(1)
    col_z_sum(2)
    col_z_sum(3)
    finish(0)
    row_z_back(0)
    row_z_back(1)
    finish(1)
    row_z_back(2)
    row_z_back(3)
    finish(2)
    finish(3)
    for c in range(CHUNKS):
        for d in x_order:
            z4(c, d, True).wait_recv()
    z_copy = pltpu.make_async_copy(z_all, z_out, z_sem)
    z_copy.start()

    for c in range(CHUNKS):
        early = c in COLUMN_FIRST
        for d in x_order:
            for p in (p1, y_over if early else p_y, p4, z4):
                p(c, d).wait_send()
        for d in y_order:
            for p in (p2, p3, z2, z3) + ((y_down,) if early else ()):
                p(c, d).wait_send()
    for copy in outs:
        copy.wait()
    z_copy.wait()


def emit(q_in, k_in, v_in, z, f, q_out, k_out, v_out, m_out, m, sem, m_sem, scale):
    copies = [
        pltpu.make_async_copy(a, b, sem.at[i])
        for i, (a, b) in enumerate(((q_in, q_out), (k_in, k_out), (v_in, v_out)))
    ]
    for copy in copies:
        copy.start()
    for part in range(4):
        for h in range(4 * part, 4 * part + 4):
            m[h] = mm(z[h], f[h]) * scale
        hs = pl.ds(4 * part, 4)
        copy = pltpu.make_async_copy(m.at[hs], m_out.at[hs], m_sem.at[part])
        copy.start()
        copies.append(copy)
    for copy in copies:
        copy.wait()


def per_device(queries, key_rows, values, out_grad, feature_map):
    tokens, width = queries.shape
    dma = pltpu.SemaphoreType.DMA
    state = (HD, HD)
    flat = jax.ShapeDtypeStruct((tokens, width), BF16)
    rows = (tokens, width)
    query_grad, key_grad, value_grad, z = pl.pallas_call(
        kernel,
        out_shape=(flat, flat, flat, jax.ShapeDtypeStruct((HEADS,) + state, BF16)),
        in_specs=[pl.BlockSpec(memory_space=pltpu.HBM)] * 5,
        out_specs=[pl.BlockSpec(memory_space=pl.ANY)] * 4,
        scratch_shapes=[
            pltpu.VMEM(rows, BF16), pltpu.VMEM(rows, BF16), pltpu.VMEM(rows, BF16), pltpu.VMEM(rows, BF16),
            pltpu.VMEM((HEADS,) + state, BF16),
            pltpu.VMEM(rows, BF16), pltpu.VMEM(rows, BF16), pltpu.VMEM(rows, BF16),
            pltpu.VMEM((NX, QUARTER, 2) + state, BF16),
            pltpu.VMEM((NX, QUARTER, 2) + state, BF16),
            pltpu.VMEM((NX, QUARTER) + state, BF16),
            pltpu.VMEM((NX, QUARTER) + state, BF16),
            pltpu.VMEM((QUARTER, 2) + state, BF16),
            pltpu.VMEM((NY, QUARTER, 2, SLICE, HD), BF16),
            pltpu.VMEM((NY, QUARTER, 2, SLICE, HD), BF16),
            pltpu.VMEM((QUARTER, 2) + state, BF16),
            pltpu.VMEM((QUARTER,) + state, F32),
            pltpu.VMEM((QUARTER,) + state, BF16),
            pltpu.VMEM((NY, QUARTER, SLICE, HD), BF16),
            pltpu.VMEM((QUARTER, SLICE, HD), BF16),
            pltpu.VMEM((QUARTER,) + state, BF16),
            pltpu.VMEM((HEADS,) + state, BF16),
            pltpu.VMEM((NY, NX, QUARTER, SLICE, HD), BF16),
            pltpu.VMEM((NX, QUARTER, SLICE, HD), BF16),
            pltpu.VMEM((NX, QUARTER, SLICE, HD), BF16),
            pltpu.VMEM((NX, QUARTER, 2) + state, BF16),
            pltpu.VMEM((HEADS, 2) + state, BF16),
            pltpu.VMEM((HEADS,) + state, BF16),
            pltpu.VMEM((HEADS,) + state, BF16),
            pltpu.VMEM((HEADS,) + state, F32), pltpu.VMEM((HEADS,) + state, F32), pltpu.VMEM((HEADS,) + state, F32),
            dma((5,)), dma((CHUNKS, NX, 3)), dma,
            *[dma((CHUNKS, NX - 1))] * 4,
            *[dma((CHUNKS, NY - 1))] * 4,
            *[dma((CHUNKS, NX - 1))] * 2,
            *[dma((CHUNKS, NY - 1))] * 4,
            *[dma((CHUNKS, NX - 1))] * 2,
            *[dma((CHUNKS, NY - 1))] * 2,
            *[dma((CHUNKS, NX - 1))] * 2,
        ],
        compiler_params=pltpu.CompilerParams(
            collective_id=0, has_side_effects=True, vmem_limit_bytes=48 * 1024 * 1024
        ),
    )(*(pltpu.with_memory_space_constraint(a, pltpu.HBM) for a in (queries, key_rows, values, out_grad, feature_map)))
    whole = pl.BlockSpec(memory_space=pltpu.VMEM)
    return pl.pallas_call(
        functools.partial(emit, scale=1.0 / math.sqrt(tokens * lax.axis_size("ctx"))),
        out_shape=(flat, flat, flat, jax.ShapeDtypeStruct((HEADS,) + state, F32)),
        in_specs=[pl.BlockSpec(memory_space=pl.ANY)] * 3 + [whole] * 2,
        out_specs=[pl.BlockSpec(memory_space=pl.ANY)] * 4,
        scratch_shapes=[pltpu.VMEM((HEADS,) + state, F32), dma((3,)), dma((4,))],
        compiler_params=pltpu.CompilerParams(vmem_limit_bytes=8 * 1024 * 1024),
    )(query_grad, key_grad, value_grad, z, feature_map)


def solution(mesh):
    placed = P(("seq", "ctx"), None)
    return jax.shard_map(
        per_device,
        mesh=mesh,
        in_specs=(placed, placed, placed, placed, P()),
        out_specs=(placed, placed, placed, P("seq", None, None)),
        check_vma=False,
    )
```

```python
import functools
import math

import jax
import jax.numpy as jnp
from jax import lax
from jax.experimental import pallas as pl
from jax.experimental.pallas import tpu as pltpu
from jax.sharding import PartitionSpec as P

MESH = pl.DeviceIdType.MESH
F32 = jnp.float32
BF16 = jnp.bfloat16

NX = 4
NY = 8
HEADS = 16
QUARTER = HEADS // NX
CHUNKS = 4
PER = QUARTER // CHUNKS
HD = 128
SLICE = HD // NY


def mm(a, b, ca=1, cb=0):
    return lax.dot_general(a, b, (((ca,), (cb,)), ((), ())), preferred_element_type=F32)


def kernel(
    q_in, k_in, v_in, g_in, f_in,
    q_out, k_out, v_out, z_out,
    q, k, v, g, f, dq, dk, dv,
    sent, got, y_sent, y_got, total, col, carry, carried,
    w_row, z_row, col_z, z_part, z_full, z_all,
    out_send, fin, h_mat, kh, aq, ak, av,
    in_sem, out_sem, z_sem,
    p1s, p1r, ys, yr, p2s, p2r, p3s, p3r, p4s, p4r, z2s, z2r, z3s, z3r, z4s, z4r,
):
    me = lax.axis_index("ctx")
    y = me // NX
    x = lax.rem(me, NX)

    def at_x(d):
        return lax.rem(x + d + NX, NX)

    def at_y(d):
        return lax.rem(y + d + NY, NY)

    def place(py, px):
        return {"ctx": py * NX + px}

    loads = [
        pltpu.make_async_copy(a, b, in_sem.at[i])
        for i, (a, b) in enumerate(((k_in, k), (v_in, v), (q_in, q), (g_in, g), (f_in, f)))
    ]
    for load in loads[:4]:
        load.start()

    barrier = pltpu.get_barrier_semaphore()
    for d in range(1, NX):
        pl.semaphore_signal(barrier, inc=1, device_id=place(y, at_x(d)), device_id_type=MESH)
    for d in range(1, NY):
        pl.semaphore_signal(barrier, inc=1, device_id=place(at_y(d), x), device_id_type=MESH)
    for load in loads[:4]:
        load.wait()
    loads[4].start()
    pl.semaphore_wait(barrier, NX + NY - 2)

    def cols(h, n=1):
        return pl.ds(pl.multiple_of(h * HD, HD), n * HD)

    def rows_of(i):
        return pl.ds(pl.multiple_of(i * SLICE, SLICE), SLICE)

    def heads_of(c):
        return range(c * PER, c * PER + PER)

    def along_x(src, dst, ssem, rsem, c, d, into):
        return pltpu.make_async_remote_copy(
            src_ref=src(at_x(d)), dst_ref=dst(at_x(-d) if into else x),
            send_sem=ssem.at[c, d - 1], recv_sem=rsem.at[c, d - 1],
            device_id=place(y, at_x(d)), device_id_type=MESH,
        )

    def along_y(src, dst, ssem, rsem, c, d, into):
        return pltpu.make_async_remote_copy(
            src_ref=src(at_y(d)), dst_ref=dst(at_y(-d) if into else y),
            send_sem=ssem.at[c, d - 1], recv_sem=rsem.at[c, d - 1],
            device_id=place(at_y(d), x), device_id_type=MESH,
        )

    def p1(c, d, into=False):
        js = pl.ds(c * PER, PER)
        return along_x(lambda i: sent.at[i, js], lambda i: got.at[i, js], p1s, p1r, c, d, into)

    def p_y(c, d, into=False):
        js = pl.ds(c * PER, PER)
        return along_x(lambda i: y_sent.at[i, js], lambda i: y_got.at[i, js], ys, yr, c, d, into)

    def p2(c, d, into=False):
        js = pl.ds(c * PER, PER)
        return along_y(lambda i: total.at[js, :, rows_of(i)], lambda i: col.at[i, js], p2s, p2r, c, d, into)

    def p3(c, d, into=False):
        js = pl.ds(c * PER, PER)
        return along_y(lambda i: carry.at[i, js], lambda i: carried.at[js, :, rows_of(i)], p3s, p3r, c, d, into)

    def p4(c, d, into=False):
        js = pl.ds(c * PER, PER)
        return along_x(
            lambda i: out_send.at[i, js], lambda i: fin.at[pl.ds(i * QUARTER + c * PER, PER)], p4s, p4r, c, d, into
        )

    def z2(c, d, into=False):
        js = pl.ds(c * PER, PER)
        return along_y(lambda i: z_row.at[js, rows_of(i)], lambda i: col_z.at[i, js], z2s, z2r, c, d, into)

    def z3(c, d, into=False):
        js = pl.ds(c * PER, PER)
        return along_y(lambda i: z_part.at[js], lambda i: z_full.at[js, rows_of(i)], z3s, z3r, c, d, into)

    def z4(c, d, into=False):
        def hs(i):
            return z_all.at[pl.ds(i * QUARTER + c * PER, PER)]

        return along_x(lambda i: hs(x), hs, z4s, z4r, c, d, into)

    x_order = (2, 1, 3)
    y_order = (4, 3, 5, 2, 6, 1, 7)

    def states(c, send=True):
        for d in x_order + (0,):
            xo = at_x(d)
            for j in heads_of(c):
                hc = cols(xo * QUARTER + j)
                ks = mm(v[:, hc], k[:, hc], 0, 0).astype(BF16)
                gs = mm(g[:, hc], q[:, hc], 0, 0).astype(BF16)
                if d:
                    sent[xo, j, 0] = ks
                    sent[xo, j, 1] = gs
                else:
                    got[x, j, 0] = ks
                    got[x, j, 1] = gs
            if d and send:
                p1(c, d).start()

    def send_states(c):
        for d in x_order:
            p1(c, d).start()

    rows = lax.broadcasted_iota(jnp.int32, (HD, HD), 0)
    columns = lax.broadcasted_iota(jnp.int32, (HD, HD), 1)
    lower = rows >= columns
    upper = rows <= columns

    def local(h):
        hc = cols(h)
        qh, kh_in, vh, gh = q[:, hc], k[:, hc], v[:, hc], g[:, hc]
        fh = f[h]
        hm = mm(fh, fh, 1, 1).astype(BF16)
        h_mat[h] = hm
        khm = mm(kh_in, hm).astype(BF16)
        kh[h] = khm
        scores_t = jnp.where(upper, mm(khm, qh, 1, 1), 0.0).astype(BF16)
        mixing = jnp.where(lower, mm(gh, vh, 1, 1), 0.0).astype(BF16)
        mixing_t = jnp.where(upper, mm(vh, gh, 1, 1), 0.0).astype(BF16)
        a = mm(mixing, kh_in)
        aq[h] = a
        ak[h] = mm(mixing_t, qh)
        av[h] = mm(scores_t, gh)
        return mm(qh, a.astype(BF16), 0, 0).astype(BF16)

    def block_work(c, d):
        xo = at_x(d)
        for j in heads_of(c):
            part = local(xo * QUARTER + j)
            if d:
                y_sent[xo, j] = part
            else:
                y_got[x, j] = part

    def send_y(c):
        for d in x_order:
            p_y(c, d).start()

    def sums(j):
        ks = [got[i, j, 0].astype(F32) for i in range(NX)]
        gs = [got[i, j, 1].astype(F32) for i in range(NX)]
        before = [None, ks[0]]
        for i in range(1, NX):
            before.append(before[-1] + ks[i])
        after = [None, gs[NX - 1]]
        for i in range(NX - 2, -1, -1):
            after.append(after[-1] + gs[i])
        return before, after

    def row_sums(c):
        for d in x_order:
            p1(c, d, True).wait_recv()
        for j in heads_of(c):
            before, after = sums(j)
            total[j, 0] = before[NX].astype(BF16)
            total[j, 1] = after[NX].astype(BF16)
            col[y, j] = total[j, :, rows_of(y)]
        for d in y_order:
            p2(c, d).start()

    def scan(c):
        for d in y_order:
            p2(c, d, True).wait_recv()
        for j in heads_of(c):
            acc = jnp.zeros((SLICE, HD), F32)
            for i in range(NY):
                carry[i, j, 0] = acc.astype(BF16)
                acc = acc + col[i, j, 0].astype(F32)
            acc = jnp.zeros((SLICE, HD), F32)
            for i in range(NY - 1, -1, -1):
                carry[i, j, 1] = acc.astype(BF16)
                acc = acc + col[i, j, 1].astype(F32)
            carried[j, :, rows_of(y)] = carry[y, j]
        for d in y_order:
            p3(c, d).start()

    def row_back(c):
        for d in y_order:
            p3(c, d, True).wait_recv()
        for j in heads_of(c):
            before, after = sums(j)
            pre = carried[j, 0].astype(F32)
            suf = carried[j, 1].astype(F32)
            for i in range(NX):
                out_send[i, j, 0] = (pre if i == 0 else pre + before[i]).astype(BF16)
                back = NX - 1 - i
                out_send[i, j, 1] = (suf if back == 0 else suf + after[back]).astype(BF16)
        for d in x_order:
            p4(c, d).start()
        fin[pl.ds(x * QUARTER + c * PER, PER)] = out_send[x, pl.ds(c * PER, PER)]

    def row_w(c):
        for j in heads_of(c):
            before, _ = sums(j)
            w = mm(got[1, j, 1], before[1].astype(BF16), 0, 0)
            for i in range(2, NX):
                w += mm(got[i, j, 1], before[i].astype(BF16), 0, 0)
            w_row[j] = w

    def row_z(c):
        for d in x_order:
            p_y(c, d, True).wait_recv()
        for j in heads_of(c):
            later = col[:, j, 1].reshape(HD, HD)
            w = w_row[j] + mm(later, carry[:, j, 0].reshape(HD, HD), 0, 0)
            for i in range(NX):
                w += y_got[i, j].astype(F32)
            z_row[j] = w.astype(BF16)
            col_z[y, j] = z_row[j, rows_of(y)]
        for d in y_order:
            z2(c, d).start()

    def col_z_sum(c):
        for d in y_order:
            z2(c, d, True).wait_recv()
        for j in heads_of(c):
            w = col_z[0, j].astype(F32)
            for i in range(1, NY):
                w += col_z[i, j].astype(F32)
            z_part[j] = w.astype(BF16)
            z_full[j, rows_of(y)] = z_part[j]
        for d in y_order:
            z3(c, d).start()

    def row_z_back(c):
        for d in y_order:
            z3(c, d, True).wait_recv()
        for j in heads_of(c):
            w = z_full[j].astype(F32)
            z_all[x * QUARTER + j] = (w + w.T).astype(BF16)
        for d in x_order:
            z4(c, d).start()

    def finish_head(h):
        hc = cols(h)
        pre_t = fin[h, 0]
        suf = fin[h, 1]
        hm = h_mat[h]
        a = (aq[h] + mm(g[:, hc], pre_t)).astype(BF16)
        dq[:, hc] = mm(a, hm).astype(BF16)
        b = (ak[h] + mm(v[:, hc], suf)).astype(BF16)
        dk[:, hc] = mm(b, hm).astype(BF16)
        dv[:, hc] = (av[h] + mm(kh[h], suf, 1, 1)).astype(BF16)

    outs = []

    def finish(c):
        places = (0, 1, 3, 2)
        for d in places[1:]:
            p4(c, d, True).wait_recv()
        for d in places:
            for j in heads_of(c):
                finish_head(at_x(-d) * QUARTER + j)
        for n, d in enumerate(places):
            part = cols(at_x(-d) * QUARTER + c * PER, PER)
            for i, (a, b) in enumerate(((dq, q_out), (dk, k_out), (dv, v_out))):
                copy = pltpu.make_async_copy(a.at[:, part], b.at[:, part], out_sem.at[c, n, i])
                copy.start()
                outs.append(copy)

    blocks = [(c, d) for c in range(CHUNKS) for d in x_order + (0,)]

    def block_span(lo, hi):
        for c, d in blocks[lo:hi]:
            block_work(c, d)

    states(0)
    states(1, False)
    states(2, False)
    states(3, False)
    loads[4].wait()
    block_span(0, 1)
    send_states(1)
    block_span(1, 5)
    send_states(2)
    row_sums(0)
    block_span(5, 8)
    send_states(3)
    row_sums(1)
    block_span(8, 12)
    scan(0)
    row_sums(2)
    send_y(0)
    block_span(12, 14)
    send_y(1)
    scan(1)
    row_sums(3)
    send_y(2)
    block_span(14, 16)
    send_y(3)
    row_back(0)
    scan(2)
    row_w(0)
    row_z(0)
    row_back(1)
    scan(3)
    row_w(1)
    row_z(1)
    row_w(2)
    row_z(2)
    row_w(3)
    row_z(3)
    row_back(2)
    col_z_sum(0)
    row_back(3)
    col_z_sum(1)
    col_z_sum(2)
    col_z_sum(3)
    finish(0)
    row_z_back(0)
    row_z_back(1)
    finish(1)
    row_z_back(2)
    row_z_back(3)
    finish(2)
    finish(3)
    for c in range(CHUNKS):
        for d in x_order:
            z4(c, d, True).wait_recv()
    z_copy = pltpu.make_async_copy(z_all, z_out, z_sem)
    z_copy.start()

    for c in range(CHUNKS):
        for d in x_order:
            for p in (p1, p_y, p4, z4):
                p(c, d).wait_send()
        for d in y_order:
            for p in (p2, p3, z2, z3):
                p(c, d).wait_send()
    for copy in outs:
        copy.wait()
    z_copy.wait()


def emit(q_in, k_in, v_in, z, f, q_out, k_out, v_out, m_out, m, sem, m_sem, scale):
    copies = [
        pltpu.make_async_copy(a, b, sem.at[i])
        for i, (a, b) in enumerate(((q_in, q_out), (k_in, k_out), (v_in, v_out)))
    ]
    for copy in copies:
        copy.start()
    for part in range(4):
        for h in range(4 * part, 4 * part + 4):
            m[h] = mm(z[h], f[h]) * scale
        hs = pl.ds(4 * part, 4)
        copy = pltpu.make_async_copy(m.at[hs], m_out.at[hs], m_sem.at[part])
        copy.start()
        copies.append(copy)
    for copy in copies:
        copy.wait()


def per_device(queries, key_rows, values, out_grad, feature_map):
    tokens, width = queries.shape
    dma = pltpu.SemaphoreType.DMA
    state = (HD, HD)
    flat = jax.ShapeDtypeStruct((tokens, width), BF16)
    rows = (tokens, width)
    query_grad, key_grad, value_grad, z = pl.pallas_call(
        kernel,
        out_shape=(flat, flat, flat, jax.ShapeDtypeStruct((HEADS,) + state, BF16)),
        in_specs=[pl.BlockSpec(memory_space=pltpu.HBM)] * 5,
        out_specs=[pl.BlockSpec(memory_space=pl.ANY)] * 4,
        scratch_shapes=[
            pltpu.VMEM(rows, BF16), pltpu.VMEM(rows, BF16), pltpu.VMEM(rows, BF16), pltpu.VMEM(rows, BF16),
            pltpu.VMEM((HEADS,) + state, BF16),
            pltpu.VMEM(rows, BF16), pltpu.VMEM(rows, BF16), pltpu.VMEM(rows, BF16),
            pltpu.VMEM((NX, QUARTER, 2) + state, BF16),
            pltpu.VMEM((NX, QUARTER, 2) + state, BF16),
            pltpu.VMEM((NX, QUARTER) + state, BF16),
            pltpu.VMEM((NX, QUARTER) + state, BF16),
            pltpu.VMEM((QUARTER, 2) + state, BF16),
            pltpu.VMEM((NY, QUARTER, 2, SLICE, HD), BF16),
            pltpu.VMEM((NY, QUARTER, 2, SLICE, HD), BF16),
            pltpu.VMEM((QUARTER, 2) + state, BF16),
            pltpu.VMEM((QUARTER,) + state, F32),
            pltpu.VMEM((QUARTER,) + state, BF16),
            pltpu.VMEM((NY, QUARTER, SLICE, HD), BF16),
            pltpu.VMEM((QUARTER, SLICE, HD), BF16),
            pltpu.VMEM((QUARTER,) + state, BF16),
            pltpu.VMEM((HEADS,) + state, BF16),
            pltpu.VMEM((NX, QUARTER, 2) + state, BF16),
            pltpu.VMEM((HEADS, 2) + state, BF16),
            pltpu.VMEM((HEADS,) + state, BF16),
            pltpu.VMEM((HEADS,) + state, BF16),
            pltpu.VMEM((HEADS,) + state, F32), pltpu.VMEM((HEADS,) + state, F32), pltpu.VMEM((HEADS,) + state, F32),
            dma((5,)), dma((CHUNKS, NX, 3)), dma,
            *[dma((CHUNKS, NX - 1))] * 4,
            *[dma((CHUNKS, NY - 1))] * 4,
            *[dma((CHUNKS, NX - 1))] * 2,
            *[dma((CHUNKS, NY - 1))] * 4,
            *[dma((CHUNKS, NX - 1))] * 2,
        ],
        compiler_params=pltpu.CompilerParams(
            collective_id=0, has_side_effects=True, vmem_limit_bytes=48 * 1024 * 1024
        ),
    )(*(pltpu.with_memory_space_constraint(a, pltpu.HBM) for a in (queries, key_rows, values, out_grad, feature_map)))
    whole = pl.BlockSpec(memory_space=pltpu.VMEM)
    return pl.pallas_call(
        functools.partial(emit, scale=1.0 / math.sqrt(tokens * lax.axis_size("ctx"))),
        out_shape=(flat, flat, flat, jax.ShapeDtypeStruct((HEADS,) + state, F32)),
        in_specs=[pl.BlockSpec(memory_space=pl.ANY)] * 3 + [whole] * 2,
        out_specs=[pl.BlockSpec(memory_space=pl.ANY)] * 4,
        scratch_shapes=[pltpu.VMEM((HEADS,) + state, F32), dma((3,)), dma((4,))],
        compiler_params=pltpu.CompilerParams(vmem_limit_bytes=8 * 1024 * 1024),
    )(query_grad, key_grad, value_grad, z, feature_map)


def solution(mesh):
    placed = P(("seq", "ctx"), None)
    return jax.shard_map(
        per_device,
        mesh=mesh,
        in_specs=(placed, placed, placed, placed, P()),
        out_specs=(placed, placed, placed, P("seq", None, None)),
        check_vma=False,
    )
```
